32 devices in a mesh: gx: 8 (over z, y), gy: 4 (over x, core).
Axes of the slice: x: 2, y: 2, z: 4, core: 2. Of those that a mesh axis runs over, the one named last changes fastest.
Arguments:
- rhs: float32 [64, 256, 256], P('gx', 'gy'), may hold values from -12 to 12
- coefs: float32 [13, 64, 256, 256], P(None, 'gx', 'gy'), may hold values from 0 to 1.4, as said below
- shifts: float32 [4], replicated, may hold values from 0.4 to 1.1
Outputs:
- basis: float32 [5, 64, 256, 256], P(None, 'gx', 'gy')
- factor: float32 [5, 5], replicated
- solution: float32 [64, 256, 256], P('gx', 'gy')
- residual: float32 [64, 256, 256], P('gx', 'gy')
The draws below stay inside these ranges and needn't reach their ends.
Inputs may be any that keep to these rules, and one draw needn't show every extreme that they name: `coefs`: entry 0 lies in 0.6 to 1.4, entries 1 to 6 in 0.02 to 0.22, entries 7 to 12 in 0 to 0.16.
All inputs are finite; a program needn't handle non-finite values.
Results may differ from the reference program's by a relative error of at most 0.00095.
Values sent between devices are 32-bit elements; how exact they have to be, the bound alone decides.
A program may use at most 64 MiB of HBM per device.

```python
import jax
import jax.numpy as jnp
from jax import lax

NZ = 256
STEPS = 4
NX = 64
NY = 256


def draw_rhs(key, part):
    noise_key, scale_key = jax.random.split(jax.random.fold_in(key, 11))
    scales = jnp.exp(jax.random.uniform(scale_key, (NX, NY, NZ), jnp.float32, jnp.log(0.1), 0.0))
    plane = jnp.arange(NX, dtype=jnp.float32)
    rising = (1.0 + 2.0 * plane / max(NX - 1, 1))[:, None, None]
    noise = jax.random.truncated_normal(noise_key, -4.0, 4.0, (NX, NY, NZ), jnp.float32)
    return noise * scales * rising


def draw_coefs(key, part):
    lower = jnp.array([0.6] + [0.02] * 6 + [0.0] * 6, jnp.float32)[:, None, None, None]
    upper = jnp.array([1.4] + [0.22] * 6 + [0.16] * 6, jnp.float32)[:, None, None, None]
    unit = jax.random.uniform(jax.random.fold_in(key, 23), (13, NX, NY, NZ), jnp.float32)
    return lower + (upper - lower) * unit


def setup_inputs(seed: int = 0) -> dict:
    splits = jax.random.split(jax.random.key(seed), 4)
    rhs = draw_rhs(jax.random.fold_in(splits[3], 71), 0)
    coefs = draw_coefs(jax.random.fold_in(splits[3], 71), 0)
    shifts = jnp.clip(jax.random.uniform(splits[2], (STEPS,), jnp.float32, 0.4, 1.1), 0.4, 1.1)
    return {"rhs": rhs, "coefs": coefs, "shifts": shifts}


growth = 2.0

def neighbours(field):
    minus_x = jnp.roll(field, 1, axis=0)
    plus_x = jnp.roll(field, -1, axis=0)
    padded = jnp.pad(field, ((0, 0), (1, 1), (1, 1)))
    minus_y = padded[:, :-2, 1:-1]
    plus_y = padded[:, 2:, 1:-1]
    minus_z = padded[:, 1:-1, :-2]
    plus_z = padded[:, 1:-1, 2:]
    return (minus_x, plus_x, minus_y, plus_y, minus_z, plus_z)

def apply_spai(field, coefs):
    total = coefs[0] * field
    near = neighbours(field)
    for index in range(6):
        total = total + coefs[1 + index] * near[index]
    return total

def apply_operator(field, coefs):
    total = field
    near = neighbours(field)
    for index in range(6):
        total = total - coefs[7 + index] * near[index]
    return total

def invert_upper(upper):
    order = upper.shape[0]
    identity = jnp.eye(order, dtype=upper.dtype)
    result = jnp.zeros_like(upper)
    for row in range(order - 1, -1, -1):
        known = identity[row] - jnp.dot(upper[row], result, precision=lax.Precision.HIGHEST)
        result = result.at[row].set(known / upper[row, row])
    return result

def least_squares(factor, shifts):
    count = shifts.shape[0]
    relation = jnp.zeros((count + 1, count), jnp.float32)
    for column in range(count):
        relation = relation.at[column, column].set(shifts[column])
        relation = relation.at[column + 1, column].set(1.0 / growth)
    hessenberg = jnp.dot(factor, relation, precision=lax.Precision.HIGHEST)
    target = factor[:, 0]
    for column in range(count):
        top = hessenberg[column]
        below = hessenberg[column + 1]
        radius = jnp.sqrt(top[column] ** 2 + below[column] ** 2)
        cosine = top[column] / radius
        sine = below[column] / radius
        hessenberg = hessenberg.at[column].set(cosine * top + sine * below)
        hessenberg = hessenberg.at[column + 1].set(cosine * below - sine * top)
        first_entry = target[column]
        second_entry = target[column + 1]
        target = target.at[column].set(cosine * first_entry + sine * second_entry)
        target = target.at[column + 1].set(cosine * second_entry - sine * first_entry)
    upper = hessenberg[:count]
    weights = jnp.dot(invert_upper(upper), target[:count], precision=lax.Precision.HIGHEST)
    combine = -jnp.dot(relation, weights, precision=lax.Precision.HIGHEST)
    combine = combine.at[0].add(1.0)
    return (weights, combine)

def reference(rhs, coefs, shifts):
    count = shifts.shape[0]
    basis_list = [rhs]
    images = []
    for step in range(count):
        image = apply_spai(basis_list[step], coefs)
        images.append(image)
        applied = apply_operator(image, coefs)
        basis_list.append(growth * (applied - shifts[step] * basis_list[step]))
    stacked = jnp.stack(basis_list)
    flat = stacked.reshape(count + 1, -1)
    gram = jnp.dot(flat, flat.T, precision=lax.Precision.HIGHEST) / flat.shape[1]
    factor = jnp.linalg.cholesky(gram).T
    inverse = invert_upper(factor)
    ortho = jnp.dot(inverse.T, flat, precision=lax.Precision.HIGHEST).reshape(stacked.shape)
    weights, combine = least_squares(factor, shifts)
    image_flat = jnp.stack(images).reshape(count, -1)
    solution = jnp.dot(weights, image_flat, precision=lax.Precision.HIGHEST).reshape(rhs.shape)
    residual = jnp.dot(combine, flat, precision=lax.Precision.HIGHEST).reshape(rhs.shape)
    return (ortho, factor, solution, residual)
```

```python
import functools

import jax
import jax.numpy as jnp
from jax import lax
from jax.experimental import pallas as pl
from jax.experimental.pallas import tpu as pltpu
from jax.sharding import PartitionSpec as P

growth = 2.0
MESH = pl.DeviceIdType.MESH
PAD = 8
ROWS = 128


def basis_kernel(
    n_gx, n_gy, shifts, rhs, coefs, v_out, w_out, gram,
    field_v, field_w, weight, part, gx_part, gy_part,
    load_sem, store_sem, xs, xr, ys, yr, gxs, gxr, gys, gyr,
):
    steps = shifts.shape[0]
    nx, ny, nz = rhs.shape
    mine = slice(1, nx + 1)
    body = slice(PAD, PAD + ny)
    gx, gy = lax.axis_index("gx"), lax.axis_index("gy")
    x_up, x_down = lax.rem(gx + 1, n_gx), lax.rem(gx + n_gx - 1, n_gx)
    has_low, has_high = gy > 0, gy < n_gy - 1

    loads = [
        pltpu.make_async_copy(rhs, field_v.at[0, mine, body, :], load_sem.at[0]),
        pltpu.make_async_copy(coefs.at[0:7], weight.at[0:7], load_sem.at[1]),
        pltpu.make_async_copy(coefs.at[7:13], weight.at[7:13], load_sem.at[2]),
    ]
    for load in loads:
        load.start()

    barrier = pltpu.get_barrier_semaphore()

    def greet_gx(d, c):
        pl.semaphore_signal(barrier, inc=1, device_id={"gx": lax.rem(gx + d, n_gx)}, device_id_type=MESH)
        return c

    def greet_gy(d, c):
        pl.semaphore_signal(barrier, inc=1, device_id={"gy": lax.rem(gy + d, n_gy)}, device_id_type=MESH)
        return c

    lax.fori_loop(1, n_gx, greet_gx, 0)
    lax.fori_loop(1, n_gy, greet_gy, 0)

    part[...] = jnp.zeros_like(part)

    def clear(fields, rows):
        for k in range(steps):
            for p in range(1, nx + 1):
                fields[k, p, rows, :] = jnp.zeros((PAD, nz), jnp.float32)

    @pl.when(jnp.logical_not(has_low))
    def _():
        clear(field_v, slice(0, PAD))
        clear(field_w, slice(0, PAD))

    @pl.when(jnp.logical_not(has_high))
    def _():
        clear(field_v, slice(PAD + ny, PAD + ny + PAD))
        clear(field_w, slice(PAD + ny, PAD + ny + PAD))

    pl.semaphore_wait(barrier, n_gx + n_gy - 2)

    def x_copy(fields, k, which, side, source=None):
        slot = 2 * steps * which + 2 * k + side
        if source is None:
            source = fields.at[k, 1 if side == 0 else nx, body, :]
        return pltpu.make_async_remote_copy(
            src_ref=source,
            dst_ref=fields.at[k, nx + 1 if side == 0 else 0, body, :],
            send_sem=xs.at[slot],
            recv_sem=xr.at[slot],
            device_id={"gx": x_down if side == 0 else x_up},
            device_id_type=MESH,
        )

    def y_copy(fields, k, which, side, source=None):
        slot = 2 * steps * which + 2 * k + side
        if source is None:
            source = fields.at[k, mine, slice(PAD, 2 * PAD) if side == 0 else slice(ny, PAD + ny), :]
        return pltpu.make_async_remote_copy(
            src_ref=source,
            dst_ref=fields.at[k, mine, slice(PAD + ny, PAD + ny + PAD) if side == 0 else slice(0, PAD), :],
            send_sem=ys.at[slot],
            recv_sem=yr.at[slot],
            device_id={"gy": jnp.maximum(gy - 1, 0) if side == 0 else jnp.minimum(gy + 1, n_gy - 1)},
            device_id_type=MESH,
        )

    def y_start(fields, k, which, sources=(None, None)):
        @pl.when(has_low)
        def _():
            y_copy(fields, k, which, 0, sources[0]).start()

        @pl.when(has_high)
        def _():
            y_copy(fields, k, which, 1, sources[1]).start()

    def y_arrived(fields, k, which):
        @pl.when(has_low)
        def _():
            y_copy(fields, k, which, 1).wait_recv()

        @pl.when(has_high)
        def _():
            y_copy(fields, k, which, 0).wait_recv()

    def near(fields, k, p, r, rows):
        centre = fields[k, p + 1, PAD + r : PAD + r + rows, :]
        lane = lax.broadcasted_iota(jnp.int32, centre.shape, 1)
        return centre, (
            fields[k, p, PAD + r : PAD + r + rows, :],
            fields[k, p + 2, PAD + r : PAD + r + rows, :],
            fields[k, p + 1, PAD + r - 1 : PAD + r - 1 + rows, :],
            fields[k, p + 1, PAD + r + 1 : PAD + r + 1 + rows, :],
            jnp.where(lane == 0, 0.0, pltpu.roll(centre, 1, 1)),
            jnp.where(lane == nz - 1, 0.0, pltpu.roll(centre, nz - 1, 1)),
        )

    chunk = 32 if ny % 32 == 0 else 8

    def plane_m(k, p):
        for r in range(0, ny, chunk):
            centre, sides = near(field_v, k, p, r, chunk)
            total = weight[0, p, r : r + chunk, :] * centre
            for d in range(6):
                total = total + weight[1 + d, p, r : r + chunk, :] * sides[d]
            field_w[k, p + 1, PAD + r : PAD + r + chunk, :] = total

    def plane_a(k, p):
        shift = shifts[k]
        for r in range(0, ny, chunk):
            centre, sides = near(field_w, k, p, r, chunk)
            total = centre
            for d in range(6):
                total = total - weight[7 + d, p, r : r + chunk, :] * sides[d]
            old = field_v[k, p + 1, PAD + r : PAD + r + chunk, :]
            field_v[k + 1, p + 1, PAD + r : PAD + r + chunk, :] = growth * (total - shift * old)

    def apply(plane, fields, k, which, out, out_k, out_which, send):
        y_arrived(fields, k, which)

        def inner(p, c):
            plane(k, p)
            return c

        lax.fori_loop(1, nx - 1, inner, 0)
        x_copy(fields, k, which, 1).wait_recv()
        plane(k, 0)

        @pl.when(send)
        def _():
            x_copy(out, out_k, out_which, 0).start()

        x_copy(fields, k, which, 0).wait_recv()
        plane(k, nx - 1)

        @pl.when(send)
        def _():
            x_copy(out, out_k, out_which, 1).start()
            y_start(out, out_k, out_which)

    def products(i):
        def one(j, c):
            def add(p, total):
                a = field_v[i, p + 1, body, :]
                b = field_v[j, p + 1, body, :]
                return total + jnp.sum((a * b).reshape(ny // 8, 8, nz), axis=0)

            total = lax.fori_loop(0, nx, add, jnp.zeros((8, nz), jnp.float32))
            row = jnp.sum(total, axis=0, keepdims=True)
            flat = row[:, :ROWS]
            for q in range(1, nz // ROWS):
                flat = flat + row[:, q * ROWS : (q + 1) * ROWS]
            part[pl.ds(i * (steps + 1) + j, 1), :] = flat
            return c

        lax.fori_loop(0, i + 1, one, 0)

    x_copy(field_v, 0, 0, 0, rhs.at[0]).start()
    x_copy(field_v, 0, 0, 1, rhs.at[nx - 1]).start()
    y_start(field_v, 0, 0, (rhs.at[:, 0:PAD, :], rhs.at[:, ny - PAD : ny, :]))
    loads[0].wait()
    products(0)
    loads[1].wait()
    loads[2].wait()

    def v_store(k):
        return pltpu.make_async_copy(field_v.at[k + 1, mine, body, :], v_out.at[k], store_sem.at[0, k])

    def w_store(k):
        return pltpu.make_async_copy(field_w.at[k, mine, body, :], w_out.at[k], store_sem.at[1, k])

    def step(k, c):
        apply(plane_m, field_v, k, 0, field_w, k, 1, k >= 0)
        w_store(k).start()
        apply(plane_a, field_w, k, 1, field_v, k + 1, 0, k + 1 < steps)
        v_store(k).start()
        products(k + 1)
        return c

    lax.fori_loop(0, steps, step, 0)

    def gather(axis, me, n, store, send_sem, recv_sem, value):
        store[me] = value

        def copy(d):
            return pltpu.make_async_remote_copy(
                src_ref=store.at[me],
                dst_ref=store.at[me],
                send_sem=send_sem.at[d],
                recv_sem=recv_sem.at[d],
                device_id={axis: lax.rem(me + d, n)},
                device_id_type=MESH,
            )

        def start(d, c):
            copy(d).start()
            return c

        def arrive(d, c):
            copy(d).wait_recv()
            return c

        def sent(d, c):
            copy(d).wait_send()
            return c

        lax.fori_loop(1, n, start, 0)
        lax.fori_loop(1, n, arrive, 0)
        total = lax.fori_loop(0, n, lambda s, t: t + store[s], jnp.zeros_like(value))
        return total, lambda: lax.fori_loop(1, n, sent, 0)

    total, done_x = gather("gx", gx, n_gx, gx_part, gxs, gxr, part[...])
    total, done_y = gather("gy", gy, n_gy, gy_part, gys, gyr, total)
    gram[...] = total
    done_x()
    done_y()

    def finish(k, c):
        for which, fields in ((0, field_v), (1, field_w)):
            for side in range(2):
                x_copy(fields, k, which, side).wait_send()

            @pl.when(has_low)
            def _():
                y_copy(fields, k, which, 0).wait_send()

            @pl.when(has_high)
            def _():
                y_copy(fields, k, which, 1).wait_send()

        v_store(k).wait()
        w_store(k).wait()
        return c

    lax.fori_loop(0, steps, finish, 0)


def small_algebra(gram, shifts, cells):
    steps = shifts.shape[0]
    order = steps + 1
    sums = jnp.sum(gram, axis=1, keepdims=True) / cells
    sums = jnp.broadcast_to(sums, gram.shape)

    def entry(i, j):
        n = max(i, j) * order + min(i, j)
        return sums[n : n + 1, :]

    factor = {}
    for i in range(order):
        value = entry(i, i)
        for k in range(i):
            value = value - factor[k, i] * factor[k, i]
        factor[i, i] = jnp.sqrt(value)
        for j in range(i + 1, order):
            value = entry(i, j)
            for k in range(i):
                value = value - factor[k, i] * factor[k, j]
            factor[i, j] = value / factor[i, i]
    inverse = {}
    for j in range(order):
        inverse[j, j] = 1.0 / factor[j, j]
        for i in range(j - 1, -1, -1):
            value = factor[i, i + 1] * inverse[i + 1, j]
            for k in range(i + 2, j + 1):
                value = value + factor[i, k] * inverse[k, j]
            inverse[i, j] = -value / factor[i, i]
    zero = jnp.zeros_like(factor[0, 0])

    def upper(i, j):
        return factor.get((i, j), zero)

    hess = [[upper(i, k) * shifts[k] + upper(i, k + 1) * (1.0 / growth) for k in range(steps)] for i in range(order)]
    target = [upper(i, 0) for i in range(order)]
    for k in range(steps):
        top, below = hess[k][k], hess[k + 1][k]
        radius = jnp.sqrt(top * top + below * below)
        cosine, sine = top / radius, below / radius
        for c in range(k, steps):
            a, b = hess[k][c], hess[k + 1][c]
            hess[k][c] = cosine * a + sine * b
            hess[k + 1][c] = cosine * b - sine * a
        a, b = target[k], target[k + 1]
        target[k] = cosine * a + sine * b
        target[k + 1] = cosine * b - sine * a
    weights = [None] * steps
    for i in range(steps - 1, -1, -1):
        value = target[i]
        for k in range(i + 1, steps):
            value = value - hess[i][k] * weights[k]
        weights[i] = value / hess[i][i]
    combine = []
    for j in range(order):
        value = zero + (1.0 if j == 0 else 0.0)
        if j < steps:
            value = value - shifts[j] * weights[j]
        if j > 0:
            value = value - (1.0 / growth) * weights[j - 1]
        combine.append(value)
    return factor, inverse, weights, combine


def combine_kernel(cells, shifts, gram, rhs, v, w, basis, factor_out, solution_out, residual, table):
    steps = shifts.shape[0]
    order = steps + 1
    pairs = [(j, k) for k in range(order) for j in range(k + 1)]
    tail = len(pairs)

    @pl.when(pl.program_id(0) == 0)
    def _():
        factor, inverse, weights, combine = small_algebra(gram[...], shifts, cells)
        values = [inverse[p] for p in pairs] + weights + combine
        for n, value in enumerate(values):
            table[n] = jnp.broadcast_to(value, table.shape[1:])
        row = lax.broadcasted_iota(jnp.int32, (8, ROWS), 0)
        column = lax.broadcasted_iota(jnp.int32, (8, ROWS), 1)
        whole = jnp.zeros((8, ROWS), jnp.float32)
        for (i, j), value in factor.items():
            whole = jnp.where((row == i) & (column == j), value, whole)
        factor_out[...] = whole[:order, :order]

    planes, ny, nz = rhs.shape

    def mul(n, x):
        return table[n][None] * x

    def tile(t, c):
        p, r = t // (ny // 16), lax.rem(t, ny // 16) * 16
        rows = pl.ds(pl.multiple_of(r, 16), 16)
        for q in range(0, nz, ROWS):
            lanes = slice(q, q + ROWS)
            at = (p, rows, lanes)
            load = lambda x: x.reshape(2, 8, ROWS)
            fields = [load(rhs[at])] + [load(v[k, p, rows, lanes]) for k in range(steps)]
            for k in range(order):
                total = None
                for j in range(k + 1):
                    term = mul(pairs.index((j, k)), fields[j])
                    total = term if total is None else total + term
                basis[k, p, rows, lanes] = total.reshape(16, ROWS)
            total = mul(tail, load(w[0, p, rows, lanes]))
            for k in range(1, steps):
                total = total + mul(tail + k, load(w[k, p, rows, lanes]))
            solution_out[at] = total.reshape(16, ROWS)
            total = mul(tail + steps, fields[0])
            for j in range(1, order):
                total = total + mul(tail + steps + j, fields[j])
            residual[at] = total.reshape(16, ROWS)
        return c

    lax.fori_loop(0, planes * (ny // 16), tile, 0)


def device_body(n_gx, n_gy, rhs, coefs, shifts):
    steps = shifts.shape[0]
    order = steps + 1
    nx, ny, nz = rhs.shape
    f32 = jnp.float32
    grown = (nx + 2, ny + 2 * PAD, nz)
    table_rows = -(-order * order // 8) * 8
    any_space = pl.BlockSpec(memory_space=pl.ANY)
    smem = pl.BlockSpec(memory_space=pltpu.SMEM)
    vmem = pl.BlockSpec(memory_space=pltpu.VMEM)
    dma = pltpu.SemaphoreType.DMA
    v, w, gram = pl.pallas_call(
        functools.partial(basis_kernel, n_gx, n_gy),
        out_shape=(
            jax.ShapeDtypeStruct((steps, nx, ny, nz), f32),
            jax.ShapeDtypeStruct((steps, nx, ny, nz), f32),
            jax.ShapeDtypeStruct((table_rows, ROWS), f32),
        ),
        in_specs=[smem, any_space, any_space],
        out_specs=(any_space, any_space, vmem),
        scratch_shapes=[
            pltpu.VMEM((order,) + grown, f32),
            pltpu.VMEM((steps,) + grown, f32),
            pltpu.VMEM(coefs.shape, f32),
            pltpu.VMEM((table_rows, ROWS), f32),
            pltpu.VMEM((n_gx, table_rows, ROWS), f32),
            pltpu.VMEM((n_gy, table_rows, ROWS), f32),
            dma((3,)),
            dma((2, steps)),
            dma((4 * steps,)),
            dma((4 * steps,)),
            dma((4 * steps,)),
            dma((4 * steps,)),
            dma((n_gx,)),
            dma((n_gx,)),
            dma((n_gy,)),
            dma((n_gy,)),
        ],
        compiler_params=pltpu.CompilerParams(
            collective_id=0, has_side_effects=True, vmem_limit_bytes=40 * 2**20
        ),
        name="basis",
    )(shifts, rhs, coefs)

    cells = float(nx * ny * nz * n_gx * n_gy)
    planes = 2 if nx % 2 == 0 else 1
    field = pl.BlockSpec((planes, ny, nz), lambda p: (p, 0, 0))
    stack = lambda count: pl.BlockSpec((count, planes, ny, nz), lambda p: (0, p, 0, 0))
    basis, factor, solved, residual = pl.pallas_call(
        functools.partial(combine_kernel, cells),
        grid=(nx // planes,),
        out_shape=(
            jax.ShapeDtypeStruct((order, nx, ny, nz), f32),
            jax.ShapeDtypeStruct((order, order), f32),
            jax.ShapeDtypeStruct((nx, ny, nz), f32),
            jax.ShapeDtypeStruct((nx, ny, nz), f32),
        ),
        in_specs=[smem, pl.BlockSpec((table_rows, ROWS), lambda p: (0, 0)), field, stack(steps), stack(steps)],
        out_specs=(stack(order), pl.BlockSpec((order, order), lambda p: (0, 0)), field, field),
        scratch_shapes=[pltpu.VMEM((order * (order + 1) // 2 + steps + order, 8, ROWS), f32)],
        compiler_params=pltpu.CompilerParams(
            dimension_semantics=("arbitrary",), vmem_limit_bytes=40 * 2**20
        ),
        name="combine",
    )(shifts, gram, rhs, v, w)
    return basis, factor, solved, residual


def solution(mesh):
    placed = (P("gx", "gy", None), P(None, "gx", "gy", None), P())
    return jax.shard_map(
        functools.partial(device_body, mesh.shape["gx"], mesh.shape["gy"]),
        mesh=mesh,
        in_specs=placed,
        out_specs=(P(None, "gx", "gy", None), P(), P("gx", "gy", None), P("gx", "gy", None)),
        check_vma=False,
    )
```

```python
import functools

import jax
import jax.numpy as jnp
from jax import lax
from jax.experimental import pallas as pl
from jax.experimental.pallas import tpu as pltpu
from jax.sharding import PartitionSpec as P

growth = 2.0
MESH = pl.DeviceIdType.MESH
PAD = 8
ROWS = 128


def basis_kernel(
    n_gx, n_gy, shifts_hbm, rhs, coefs, v_out, w_out, gram,
    field_v, field_w, weight, part, gx_part, gy_part, shifts, y_out, y_in,
    load_sem, store_sem, xs, xr, ys, yr, gxs, gxr, gys, gyr,
):
    steps = shifts.shape[0]
    nx, ny, nz = rhs.shape
    mine = slice(1, nx + 1)
    body = slice(PAD, PAD + ny)
    gx, gy = lax.axis_index("gx"), lax.axis_index("gy")
    x_up, x_down = lax.rem(gx + 1, n_gx), lax.rem(gx + n_gx - 1, n_gx)
    has_low, has_high = gy > 0, gy < n_gy - 1

    loads = [
        pltpu.make_async_copy(rhs, field_v.at[0, mine, body, :], load_sem.at[0]),
        pltpu.make_async_copy(coefs.at[0:7], weight.at[0:7], load_sem.at[1]),
        pltpu.make_async_copy(coefs.at[7:13], weight.at[7:13], load_sem.at[2]),
        pltpu.make_async_copy(shifts_hbm, shifts, load_sem.at[3]),
    ]
    for load in loads:
        load.start()

    barrier = pltpu.get_barrier_semaphore()

    def greet_gx(d, c):
        pl.semaphore_signal(barrier, inc=1, device_id={"gx": lax.rem(gx + d, n_gx)}, device_id_type=MESH)
        return c

    def greet_gy(d, c):
        pl.semaphore_signal(barrier, inc=1, device_id={"gy": lax.rem(gy + d, n_gy)}, device_id_type=MESH)
        return c

    lax.fori_loop(1, n_gx, greet_gx, 0)
    lax.fori_loop(1, n_gy, greet_gy, 0)

    part[...] = jnp.zeros_like(part)

    def clear(fields, rows):
        for k in range(steps):
            for p in range(1, nx + 1):
                fields[k, p, rows, :] = jnp.zeros((PAD, nz), jnp.float32)

    @pl.when(jnp.logical_not(has_low))
    def _():
        clear(field_v, slice(0, PAD))
        clear(field_w, slice(0, PAD))

    @pl.when(jnp.logical_not(has_high))
    def _():
        clear(field_v, slice(PAD + ny, PAD + ny + PAD))
        clear(field_w, slice(PAD + ny, PAD + ny + PAD))

    pl.semaphore_wait(barrier, n_gx + n_gy - 2)

    chunk = ny // 4 if ny % 32 == 0 else ny
    pieces = ny // chunk
    order = [c for c in range(pieces) if 0 < c < pieces - 1] + sorted({0, pieces - 1})

    def x_copy(fields, k, which, side, c, source=None):
        slot = pieces * (2 * steps * which + 2 * k + side) + c
        rows = slice(PAD + c * chunk, PAD + (c + 1) * chunk)
        if source is None:
            source = fields.at[k, 1 if side == 0 else nx, rows, :]
        return pltpu.make_async_remote_copy(
            src_ref=source,
            dst_ref=fields.at[k, nx + 1 if side == 0 else 0, rows, :],
            send_sem=xs.at[slot],
            recv_sem=xr.at[slot],
            device_id={"gx": x_down if side == 0 else x_up},
            device_id_type=MESH,
        )

    def y_copy(k, which, side):
        slot = 2 * steps * which + 2 * k + side
        return pltpu.make_async_remote_copy(
            src_ref=y_out.at[slot],
            dst_ref=y_in.at[slot],
            send_sem=ys.at[slot],
            recv_sem=yr.at[slot],
            device_id={"gy": jnp.maximum(gy - 1, 0) if side == 0 else jnp.minimum(gy + 1, n_gy - 1)},
            device_id_type=MESH,
        )

    def y_start(fields, k, which):
        for side, there in ((0, has_low), (1, has_high)):
            slot = 2 * steps * which + 2 * k + side
            row = PAD if side == 0 else PAD + ny - 1

            @pl.when(there)
            def _():
                for p in range(nx):
                    y_out[slot, p : p + 1, :] = fields[k, p + 1, row : row + 1, :]
                y_copy(k, which, side).start()

    def y_arrived(fields, k, which):
        for side, there in ((1, has_low), (0, has_high)):
            slot = 2 * steps * which + 2 * k + side
            row = PAD + ny if side == 0 else PAD - 1

            @pl.when(there)
            def _():
                y_copy(k, which, side).wait_recv()
                for p in range(nx):
                    fields[k, p + 1, row : row + 1, :] = y_in[slot, p : p + 1, :]

    def near(fields, k, p, r, rows):
        centre = fields[k, p + 1, PAD + r : PAD + r + rows, :]
        lane = lax.broadcasted_iota(jnp.int32, centre.shape, 1)
        return centre, (
            fields[k, p, PAD + r : PAD + r + rows, :],
            fields[k, p + 2, PAD + r : PAD + r + rows, :],
            fields[k, p + 1, PAD + r - 1 : PAD + r - 1 + rows, :],
            fields[k, p + 1, PAD + r + 1 : PAD + r + 1 + rows, :],
            jnp.where(lane == 0, 0.0, pltpu.roll(centre, 1, 1)),
            jnp.where(lane == nz - 1, 0.0, pltpu.roll(centre, nz - 1, 1)),
        )

    def block_m(k, p, r, rows):
        centre, sides = near(field_v, k, p, r, rows)
        total = weight[0, p, r : r + rows, :] * centre
        for d in range(6):
            total = total + weight[1 + d, p, r : r + rows, :] * sides[d]
        field_w[k, p + 1, PAD + r : PAD + r + rows, :] = total

    def block_a(k, p, r, rows):
        centre, sides = near(field_w, k, p, r, rows)
        total = centre
        for d in range(6):
            total = total - weight[7 + d, p, r : r + rows, :] * sides[d]
        old = field_v[k, p + 1, PAD + r : PAD + r + rows, :]
        field_v[k + 1, p + 1, PAD + r : PAD + r + rows, :] = growth * (total - shifts[k] * old)

    def apply(block, fields, k, which, out, out_k, out_which, send):
        for c in order:
            if c == 0:
                y_arrived(fields, k, which)
            for side in range(2):
                x_copy(fields, k, which, 1 - side, c).wait_recv()
                block(k, 0 if side == 0 else nx - 1, c * chunk, chunk)

                @pl.when(send)
                def _():
                    x_copy(out, out_k, out_which, side, c).start()

        def edge(p, c):
            block(k, p, 0, 8)
            block(k, p, ny - 8, 8)
            return c

        lax.fori_loop(1, nx - 1, edge, 0)

        @pl.when(send)
        def _():
            y_start(out, out_k, out_which)

        def inner(p, c):
            for r in range(8, ny - 8, 16):
                block(k, p, r, min(16, ny - 8 - r))
            return c

        lax.fori_loop(1, nx - 1, inner, 0)

    def products(i):
        def one(j, c):
            def add(p, total):
                a = field_v[i, p + 1, body, :]
                b = field_v[j, p + 1, body, :]
                return total + jnp.sum((a * b).reshape(ny // 8, 8, nz), axis=0)

            total = lax.fori_loop(0, nx, add, jnp.zeros((8, nz), jnp.float32))
            row = jnp.sum(total, axis=0, keepdims=True)
            flat = row[:, :ROWS]
            for q in range(1, nz // ROWS):
                flat = flat + row[:, q * ROWS : (q + 1) * ROWS]
            part[pl.ds(i * (i + 1) // 2 + j, 1), :] = flat
            return c

        lax.fori_loop(0, i + 1, one, 0)

    for c in order:
        for side in range(2):
            plane = rhs.at[0 if side == 0 else nx - 1, c * chunk : (c + 1) * chunk, :]
            x_copy(field_v, 0, 0, side, c, plane).start()
    loads[0].wait()
    y_start(field_v, 0, 0)
    products(0)
    for load in loads[1:]:
        load.wait()

    def v_store(k):
        return pltpu.make_async_copy(field_v.at[k, mine, body, :], v_out.at[k], store_sem.at[0, k])

    def w_store(k):
        return pltpu.make_async_copy(field_w.at[k, mine, body, :], w_out.at[k], store_sem.at[1, k])

    def step(k, c):
        apply(block_m, field_v, k, 0, field_w, k, 1, k >= 0)
        w_store(k).start()
        apply(block_a, field_w, k, 1, field_v, k + 1, 0, k + 1 < steps)
        v_store(k + 1).start()
        products(k + 1)
        return c

    v_store(0).start()
    lax.fori_loop(0, steps, step, 0)

    def gather(axis, me, n, store, send_sem, recv_sem, value):
        store[me] = value

        def copy(d):
            return pltpu.make_async_remote_copy(
                src_ref=store.at[me],
                dst_ref=store.at[me],
                send_sem=send_sem.at[d],
                recv_sem=recv_sem.at[d],
                device_id={axis: lax.rem(me + d, n)},
                device_id_type=MESH,
            )

        def start(d, c):
            copy(d).start()
            return c

        def arrive(d, c):
            copy(d).wait_recv()
            return c

        def sent(d, c):
            copy(d).wait_send()
            return c

        lax.fori_loop(1, n, start, 0)
        lax.fori_loop(1, n, arrive, 0)
        total = lax.fori_loop(0, n, lambda s, t: t + store[s], jnp.zeros_like(value))
        return total, lambda: lax.fori_loop(1, n, sent, 0)

    half = part.shape[0] // 2
    sums = jnp.sum(part[...], axis=1, keepdims=True)
    left = lax.broadcasted_iota(jnp.int32, (half, ROWS), 1) < ROWS // 2
    packed = jnp.where(left, jnp.broadcast_to(sums[:half], left.shape), jnp.broadcast_to(sums[half:], left.shape))
    total, done_x = gather("gx", gx, n_gx, gx_part, gxs, gxr, packed)
    total, done_y = gather("gy", gy, n_gy, gy_part, gys, gyr, total)
    gram[0:half, :] = total
    for k in range(steps):
        gram[half + k : half + k + 1, :] = jnp.full((1, ROWS), shifts[k], jnp.float32)
    done_x()
    done_y()

    def finish(k, c):
        for which, fields in ((0, field_v), (1, field_w)):
            for side in range(2):
                for piece in range(pieces):
                    x_copy(fields, k, which, side, piece).wait_send()

            @pl.when(has_low)
            def _():
                y_copy(k, which, 0).wait_send()

            @pl.when(has_high)
            def _():
                y_copy(k, which, 1).wait_send()

        v_store(k).wait()
        w_store(k).wait()
        return c

    lax.fori_loop(0, steps, finish, 0)
    v_store(steps).wait()


def small_algebra(gram, steps, cells):
    order = steps + 1
    half = gram.shape[0] // 2
    shifts = [gram[half + k : half + k + 1, :] for k in range(steps)]
    sums = gram[:half] / cells
    turned = pltpu.roll(sums, ROWS // 2, 1)
    left = lax.broadcasted_iota(jnp.int32, sums.shape, 1) < ROWS // 2
    sums = (jnp.where(left, sums, turned), jnp.where(left, turned, sums))

    def entry(i, j):
        n = max(i, j) * (max(i, j) + 1) // 2 + min(i, j)
        return sums[n // half][n % half : n % half + 1, :]

    factor = {}
    for i in range(order):
        value = entry(i, i)
        for k in range(i):
            value = value - factor[k, i] * factor[k, i]
        factor[i, i] = jnp.sqrt(value)
        for j in range(i + 1, order):
            value = entry(i, j)
            for k in range(i):
                value = value - factor[k, i] * factor[k, j]
            factor[i, j] = value / factor[i, i]
    inverse = {}
    for j in range(order):
        inverse[j, j] = 1.0 / factor[j, j]
        for i in range(j - 1, -1, -1):
            value = factor[i, i + 1] * inverse[i + 1, j]
            for k in range(i + 2, j + 1):
                value = value + factor[i, k] * inverse[k, j]
            inverse[i, j] = -value / factor[i, i]
    zero = jnp.zeros_like(factor[0, 0])

    def upper(i, j):
        return factor.get((i, j), zero)

    hess = [[upper(i, k) * shifts[k] + upper(i, k + 1) * (1.0 / growth) for k in range(steps)] for i in range(order)]
    target = [upper(i, 0) for i in range(order)]
    for k in range(steps):
        top, below = hess[k][k], hess[k + 1][k]
        radius = jnp.sqrt(top * top + below * below)
        cosine, sine = top / radius, below / radius
        for c in range(k, steps):
            a, b = hess[k][c], hess[k + 1][c]
            hess[k][c] = cosine * a + sine * b
            hess[k + 1][c] = cosine * b - sine * a
        a, b = target[k], target[k + 1]
        target[k] = cosine * a + sine * b
        target[k + 1] = cosine * b - sine * a
    weights = [None] * steps
    for i in range(steps - 1, -1, -1):
        value = target[i]
        for k in range(i + 1, steps):
            value = value - hess[i][k] * weights[k]
        weights[i] = value / hess[i][i]
    combine = []
    for j in range(order):
        value = zero + (1.0 if j == 0 else 0.0)
        if j < steps:
            value = value - shifts[j] * weights[j]
        if j > 0:
            value = value - (1.0 / growth) * weights[j - 1]
        combine.append(value)
    return factor, inverse, weights, combine


def combine_kernel(cells, gram, v, w, basis, factor_out, solution_out, residual, table, basis_v, sol_v, res_v, sem):
    order, nx, ny, nz = v.shape
    steps = order - 1
    pairs = [(j, k) for k in range(order) for j in range(k + 1)]
    tail = len(pairs)

    factor, inverse, weights, combine = small_algebra(gram[...], steps, cells)
    values = [inverse[p] for p in pairs] + weights + combine
    for n, value in enumerate(values):
        table[n] = jnp.broadcast_to(value, table.shape[1:])
    row = lax.broadcasted_iota(jnp.int32, (8, ROWS), 0)
    column = lax.broadcasted_iota(jnp.int32, (8, ROWS), 1)
    whole = jnp.zeros((8, ROWS), jnp.float32)
    for (i, j), value in factor.items():
        whole = jnp.where((row == i) & (column == j), value, whole)
    factor_out[...] = whole[:order, :order]

    def mul(n, x):
        return table[n][None] * x

    deep = 16 if ny % 16 == 0 else 8

    def tile(p, t):
        rows = pl.ds(pl.multiple_of(t * deep, deep), deep)
        for q in range(0, nz, ROWS):
            lanes = slice(q, q + ROWS)
            load = lambda x: x.reshape(deep // 8, 8, ROWS)
            fields = [load(v[k, p, rows, lanes]) for k in range(order)]
            for k in range(order):
                total = None
                for j in range(k + 1):
                    term = mul(pairs.index((j, k)), fields[j])
                    total = term if total is None else total + term
                basis_v[k, p, rows, lanes] = total.reshape(deep, ROWS)
            total = mul(tail, load(w[0, p, rows, lanes]))
            for k in range(1, steps):
                total = total + mul(tail + k, load(w[k, p, rows, lanes]))
            sol_v[p, rows, lanes] = total.reshape(deep, ROWS)
            total = mul(tail + steps, fields[0])
            for j in range(1, order):
                total = total + mul(tail + steps + j, fields[j])
            res_v[p, rows, lanes] = total.reshape(deep, ROWS)

    def copies(p):
        return (
            pltpu.make_async_copy(basis_v.at[:, p], basis.at[:, p], sem.at[p, 0]),
            pltpu.make_async_copy(sol_v.at[p], solution_out.at[p], sem.at[p, 1]),
            pltpu.make_async_copy(res_v.at[p], residual.at[p], sem.at[p, 2]),
        )

    def plane(p, c):
        def inner(t, d):
            tile(p, t)
            return d

        lax.fori_loop(0, ny // deep, inner, 0)
        for copy in copies(p):
            copy.start()
        return c

    def finish(p, c):
        for copy in copies(p):
            copy.wait()
        return c

    lax.fori_loop(0, nx, plane, 0)
    lax.fori_loop(0, nx, finish, 0)


def device_body(n_gx, n_gy, rhs, coefs, shifts):
    steps = shifts.shape[0]
    order = steps + 1
    nx, ny, nz = rhs.shape
    f32 = jnp.float32
    grown = (nx + 2, ny + 2 * PAD, nz)
    half = -(-(order * (order + 1) // 2) // 16) * 8
    pieces = 4 if ny % 32 == 0 else 1
    hbm = pl.BlockSpec(memory_space=pltpu.HBM)
    any_space = pl.BlockSpec(memory_space=pl.ANY)
    vmem = pl.BlockSpec(memory_space=pltpu.VMEM)
    dma = pltpu.SemaphoreType.DMA
    halo = 4 * steps
    rhs = pltpu.with_memory_space_constraint(rhs, pltpu.HBM)
    coefs = pltpu.with_memory_space_constraint(coefs, pltpu.HBM)
    shifts = pltpu.with_memory_space_constraint(shifts, pltpu.HBM)
    v, w, gram = pl.pallas_call(
        functools.partial(basis_kernel, n_gx, n_gy),
        out_shape=(
            jax.ShapeDtypeStruct((order, nx, ny, nz), f32),
            jax.ShapeDtypeStruct((steps, nx, ny, nz), f32),
            jax.ShapeDtypeStruct((2 * half, ROWS), f32),
        ),
        in_specs=[hbm, hbm, hbm],
        out_specs=(any_space, any_space, vmem),
        scratch_shapes=[
            pltpu.VMEM((order,) + grown, f32),
            pltpu.VMEM((steps,) + grown, f32),
            pltpu.VMEM(coefs.shape, f32),
            pltpu.VMEM((2 * half, ROWS), f32),
            pltpu.VMEM((n_gx, half, ROWS), f32),
            pltpu.VMEM((n_gy, half, ROWS), f32),
            pltpu.SMEM(shifts.shape, f32),
            pltpu.VMEM((halo, nx, nz), f32),
            pltpu.VMEM((halo, nx, nz), f32),
            dma((4,)),
            dma((2, order)),
            dma((halo * pieces,)),
            dma((halo * pieces,)),
            dma((halo,)),
            dma((halo,)),
            dma((n_gx,)),
            dma((n_gx,)),
            dma((n_gy,)),
            dma((n_gy,)),
        ],
        compiler_params=pltpu.CompilerParams(
            collective_id=0, has_side_effects=True, vmem_limit_bytes=32 * 2**20
        ),
        name="basis",
    )(shifts, rhs, coefs)

    cells = float(nx * ny * nz * n_gx * n_gy)
    return pl.pallas_call(
        functools.partial(combine_kernel, cells),
        out_shape=(
            jax.ShapeDtypeStruct((order, nx, ny, nz), f32),
            jax.ShapeDtypeStruct((order, order), f32),
            jax.ShapeDtypeStruct((nx, ny, nz), f32),
            jax.ShapeDtypeStruct((nx, ny, nz), f32),
        ),
        in_specs=[vmem, vmem, vmem],
        out_specs=(hbm, vmem, hbm, hbm),
        scratch_shapes=[
            pltpu.VMEM((order * (order + 1) // 2 + steps + order, 8, ROWS), f32),
            pltpu.VMEM((order, nx, ny, nz), f32),
            pltpu.VMEM((nx, ny, nz), f32),
            pltpu.VMEM((nx, ny, nz), f32),
            dma((nx, 3)),
        ],
        compiler_params=pltpu.CompilerParams(vmem_limit_bytes=32 * 2**20),
        name="combine",
    )(gram, v, w)


def solution(mesh):
    placed = (P("gx", "gy", None), P(None, "gx", "gy", None), P())
    return jax.shard_map(
        functools.partial(device_body, mesh.shape["gx"], mesh.shape["gy"]),
        mesh=mesh,
        in_specs=placed,
        out_specs=(P(None, "gx", "gy", None), P(), P("gx", "gy", None), P("gx", "gy", None)),
        check_vma=False,
    )
```

```python
import functools

import jax
import jax.numpy as jnp
from jax import lax
from jax.experimental import pallas as pl
from jax.experimental.pallas import tpu as pltpu
from jax.sharding import PartitionSpec as P

growth = 2.0
MESH = pl.DeviceIdType.MESH
PAD = 8
ROWS = 128


def basis_kernel(
    n_gx, n_gy, shifts_hbm, rhs, coefs, v_out, w_out, gram,
    field_v, field_w, weight, part, gx_part, gy_part, shifts, y_out, y_in,
    load_sem, store_sem, xs, xr, ys, yr, gxs, gxr, gys, gyr,
):
    steps = shifts.shape[0]
    nx, ny, nz = rhs.shape
    mine = slice(1, nx + 1)
    body = slice(PAD, PAD + ny)
    gx, gy = lax.axis_index("gx"), lax.axis_index("gy")
    x_up, x_down = lax.rem(gx + 1, n_gx), lax.rem(gx + n_gx - 1, n_gx)
    has_low, has_high = gy > 0, gy < n_gy - 1

    loads = [
        pltpu.make_async_copy(rhs, field_v.at[0, mine, body, :], load_sem.at[0]),
        pltpu.make_async_copy(coefs.at[0:7], weight.at[0:7], load_sem.at[1]),
        pltpu.make_async_copy(coefs.at[7:13], weight.at[7:13], load_sem.at[2]),
        pltpu.make_async_copy(shifts_hbm, shifts, load_sem.at[3]),
    ]
    for load in loads:
        load.start()

    barrier = pltpu.get_barrier_semaphore()

    def greet_gx(d, c):
        pl.semaphore_signal(barrier, inc=1, device_id={"gx": lax.rem(gx + d, n_gx)}, device_id_type=MESH)
        return c

    def greet_gy(d, c):
        pl.semaphore_signal(barrier, inc=1, device_id={"gy": lax.rem(gy + d, n_gy)}, device_id_type=MESH)
        return c

    lax.fori_loop(1, n_gx, greet_gx, 0)
    lax.fori_loop(1, n_gy, greet_gy, 0)

    part[...] = jnp.zeros_like(part)

    def clear(fields, rows):
        for k in range(steps):
            for p in range(1, nx + 1):
                fields[k, p, rows, :] = jnp.zeros((PAD, nz), jnp.float32)

    @pl.when(jnp.logical_not(has_low))
    def _():
        clear(field_v, slice(0, PAD))
        clear(field_w, slice(0, PAD))

    @pl.when(jnp.logical_not(has_high))
    def _():
        clear(field_v, slice(PAD + ny, PAD + ny + PAD))
        clear(field_w, slice(PAD + ny, PAD + ny + PAD))

    pl.semaphore_wait(barrier, n_gx + n_gy - 2)

    chunk = ny // 4 if ny % 32 == 0 else ny
    pieces = ny // chunk
    order = [c for c in range(pieces) if 0 < c < pieces - 1] + sorted({0, pieces - 1})

    def x_copy(fields, k, which, side, c, source=None):
        slot = pieces * (2 * steps * which + 2 * k + side) + c
        rows = slice(PAD + c * chunk, PAD + (c + 1) * chunk)
        if source is None:
            source = fields.at[k, 1 if side == 0 else nx, rows, :]
        return pltpu.make_async_remote_copy(
            src_ref=source,
            dst_ref=fields.at[k, nx + 1 if side == 0 else 0, rows, :],
            send_sem=xs.at[slot],
            recv_sem=xr.at[slot],
            device_id={"gx": x_down if side == 0 else x_up},
            device_id_type=MESH,
        )

    def y_copy(k, which, side):
        slot = 2 * steps * which + 2 * k + side
        return pltpu.make_async_remote_copy(
            src_ref=y_out.at[slot],
            dst_ref=y_in.at[slot],
            send_sem=ys.at[slot],
            recv_sem=yr.at[slot],
            device_id={"gy": jnp.maximum(gy - 1, 0) if side == 0 else jnp.minimum(gy + 1, n_gy - 1)},
            device_id_type=MESH,
        )

    def y_start(fields, k, which):
        for side, there in ((0, has_low), (1, has_high)):
            slot = 2 * steps * which + 2 * k + side
            row = PAD if side == 0 else PAD + ny - 1

            @pl.when(there)
            def _():
                for p in range(nx):
                    y_out[slot, p : p + 1, :] = fields[k, p + 1, row : row + 1, :]
                y_copy(k, which, side).start()

    def y_arrived(fields, k, which):
        for side, there in ((1, has_low), (0, has_high)):
            slot = 2 * steps * which + 2 * k + side
            row = PAD + ny if side == 0 else PAD - 1

            @pl.when(there)
            def _():
                y_copy(k, which, side).wait_recv()
                for p in range(nx):
                    fields[k, p + 1, row : row + 1, :] = y_in[slot, p : p + 1, :]

    def near(fields, k, p, r, rows):
        centre = fields[k, p + 1, PAD + r : PAD + r + rows, :]
        lane = lax.broadcasted_iota(jnp.int32, centre.shape, 1)
        return centre, (
            fields[k, p, PAD + r : PAD + r + rows, :],
            fields[k, p + 2, PAD + r : PAD + r + rows, :],
            fields[k, p + 1, PAD + r - 1 : PAD + r - 1 + rows, :],
            fields[k, p + 1, PAD + r + 1 : PAD + r + 1 + rows, :],
            jnp.where(lane == 0, 0.0, pltpu.roll(centre, 1, 1)),
            jnp.where(lane == nz - 1, 0.0, pltpu.roll(centre, nz - 1, 1)),
        )

    def block_m(k, p, r, rows):
        centre, sides = near(field_v, k, p, r, rows)
        total = weight[0, p, r : r + rows, :] * centre
        for d in range(6):
            total = total + weight[1 + d, p, r : r + rows, :] * sides[d]
        field_w[k, p + 1, PAD + r : PAD + r + rows, :] = total

    def block_a(k, p, r, rows):
        centre, sides = near(field_w, k, p, r, rows)
        total = centre
        for d in range(6):
            total = total - weight[7 + d, p, r : r + rows, :] * sides[d]
        old = field_v[k, p + 1, PAD + r : PAD + r + rows, :]
        field_v[k + 1, p + 1, PAD + r : PAD + r + rows, :] = growth * (total - shifts[k] * old)

    def apply(block, fields, k, which, out, out_k, out_which, send):
        y_arrived(fields, k, which)

        def edge(p, c):
            block(k, p, 0, 8)
            block(k, p, ny - 8, 8)
            return c

        lax.fori_loop(1, nx - 1, edge, 0)

        for c in order:
            for side in range(2):
                x_copy(fields, k, which, 1 - side, c).wait_recv()
                block(k, 0 if side == 0 else nx - 1, c * chunk, chunk)

                @pl.when(send)
                def _():
                    x_copy(out, out_k, out_which, side, c).start()

        @pl.when(send)
        def _():
            y_start(out, out_k, out_which)

        def inner(p, c):
            for r in range(8, ny - 8, 16):
                block(k, p, r, min(16, ny - 8 - r))
            return c

        lax.fori_loop(1, nx - 1, inner, 0)

    def products(i):
        def one(j, c):
            def add(p, total):
                a = field_v[i, p + 1, body, :]
                b = field_v[j, p + 1, body, :]
                return total + jnp.sum((a * b).reshape(ny // 8, 8, nz), axis=0)

            total = lax.fori_loop(0, nx, add, jnp.zeros((8, nz), jnp.float32))
            row = jnp.sum(total, axis=0, keepdims=True)
            flat = row[:, :ROWS]
            for q in range(1, nz // ROWS):
                flat = flat + row[:, q * ROWS : (q + 1) * ROWS]
            part[pl.ds(i * (i + 1) // 2 + j, 1), :] = flat
            return c

        lax.fori_loop(0, i + 1, one, 0)

    for c in order:
        for side in range(2):
            plane = rhs.at[0 if side == 0 else nx - 1, c * chunk : (c + 1) * chunk, :]
            x_copy(field_v, 0, 0, side, c, plane).start()
    loads[0].wait()
    y_start(field_v, 0, 0)
    products(0)
    for load in loads[1:]:
        load.wait()

    def v_store(k):
        return pltpu.make_async_copy(field_v.at[k, mine, body, :], v_out.at[k], store_sem.at[0, k])

    def w_store(k):
        return pltpu.make_async_copy(field_w.at[k, mine, body, :], w_out.at[k], store_sem.at[1, k])

    def step(k, c):
        apply(block_m, field_v, k, 0, field_w, k, 1, k >= 0)
        w_store(k).start()
        apply(block_a, field_w, k, 1, field_v, k + 1, 0, k + 1 < steps)
        v_store(k + 1).start()
        products(k + 1)
        return c

    v_store(0).start()
    lax.fori_loop(0, steps, step, 0)

    def gather(axis, me, n, store, send_sem, recv_sem, value):
        store[me] = value

        def copy(d):
            return pltpu.make_async_remote_copy(
                src_ref=store.at[me],
                dst_ref=store.at[me],
                send_sem=send_sem.at[d],
                recv_sem=recv_sem.at[d],
                device_id={axis: lax.rem(me + d, n)},
                device_id_type=MESH,
            )

        def start(d, c):
            copy(d).start()
            return c

        def arrive(d, c):
            copy(d).wait_recv()
            return c

        def sent(d, c):
            copy(d).wait_send()
            return c

        lax.fori_loop(1, n, start, 0)
        lax.fori_loop(1, n, arrive, 0)
        total = lax.fori_loop(0, n, lambda s, t: t + store[s], jnp.zeros_like(value))
        return total, lambda: lax.fori_loop(1, n, sent, 0)

    half = part.shape[0] // 2
    sums = jnp.sum(part[...], axis=1, keepdims=True)
    left = lax.broadcasted_iota(jnp.int32, (half, ROWS), 1) < ROWS // 2
    packed = jnp.where(left, jnp.broadcast_to(sums[:half], left.shape), jnp.broadcast_to(sums[half:], left.shape))
    total, done_x = gather("gx", gx, n_gx, gx_part, gxs, gxr, packed)
    total, done_y = gather("gy", gy, n_gy, gy_part, gys, gyr, total)
    gram[0:half, :] = total
    for k in range(steps):
        gram[half + k : half + k + 1, :] = jnp.full((1, ROWS), shifts[k], jnp.float32)
    done_x()
    done_y()

    def finish(k, c):
        for which, fields in ((0, field_v), (1, field_w)):
            for side in range(2):
                for piece in range(pieces):
                    x_copy(fields, k, which, side, piece).wait_send()

            @pl.when(has_low)
            def _():
                y_copy(k, which, 0).wait_send()

            @pl.when(has_high)
            def _():
                y_copy(k, which, 1).wait_send()

        v_store(k).wait()
        w_store(k).wait()
        return c

    lax.fori_loop(0, steps, finish, 0)
    v_store(steps).wait()


def small_algebra(gram, steps, cells):
    order = steps + 1
    half = gram.shape[0] // 2
    shifts = [gram[half + k : half + k + 1, :] for k in range(steps)]
    sums = gram[:half] / cells
    turned = pltpu.roll(sums, ROWS // 2, 1)
    left = lax.broadcasted_iota(jnp.int32, sums.shape, 1) < ROWS // 2
    sums = (jnp.where(left, sums, turned), jnp.where(left, turned, sums))

    def entry(i, j):
        n = max(i, j) * (max(i, j) + 1) // 2 + min(i, j)
        return sums[n // half][n % half : n % half + 1, :]

    factor = {}
    for i in range(order):
        value = entry(i, i)
        for k in range(i):
            value = value - factor[k, i] * factor[k, i]
        factor[i, i] = jnp.sqrt(value)
        for j in range(i + 1, order):
            value = entry(i, j)
            for k in range(i):
                value = value - factor[k, i] * factor[k, j]
            factor[i, j] = value / factor[i, i]
    inverse = {}
    for j in range(order):
        inverse[j, j] = 1.0 / factor[j, j]
        for i in range(j - 1, -1, -1):
            value = factor[i, i + 1] * inverse[i + 1, j]
            for k in range(i + 2, j + 1):
                value = value + factor[i, k] * inverse[k, j]
            inverse[i, j] = -value / factor[i, i]
    zero = jnp.zeros_like(factor[0, 0])

    def upper(i, j):
        return factor.get((i, j), zero)

    hess = [[upper(i, k) * shifts[k] + upper(i, k + 1) * (1.0 / growth) for k in range(steps)] for i in range(order)]
    target = [upper(i, 0) for i in range(order)]
    for k in range(steps):
        top, below = hess[k][k], hess[k + 1][k]
        radius = jnp.sqrt(top * top + below * below)
        cosine, sine = top / radius, below / radius
        for c in range(k, steps):
            a, b = hess[k][c], hess[k + 1][c]
            hess[k][c] = cosine * a + sine * b
            hess[k + 1][c] = cosine * b - sine * a
        a, b = target[k], target[k + 1]
        target[k] = cosine * a + sine * b
        target[k + 1] = cosine * b - sine * a
    weights = [None] * steps
    for i in range(steps - 1, -1, -1):
        value = target[i]
        for k in range(i + 1, steps):
            value = value - hess[i][k] * weights[k]
        weights[i] = value / hess[i][i]
    combine = []
    for j in range(order):
        value = zero + (1.0 if j == 0 else 0.0)
        if j < steps:
            value = value - shifts[j] * weights[j]
        if j > 0:
            value = value - (1.0 / growth) * weights[j - 1]
        combine.append(value)
    return factor, inverse, weights, combine


def combine_kernel(cells, gram, v, w, basis, factor_out, solution_out, residual, table, basis_v, sol_v, res_v, sem):
    order, nx, ny, nz = v.shape
    steps = order - 1
    pairs = [(j, k) for k in range(order) for j in range(k + 1)]
    tail = len(pairs)

    factor, inverse, weights, combine = small_algebra(gram[...], steps, cells)
    values = [inverse[p] for p in pairs] + weights + combine
    for n, value in enumerate(values):
        table[n] = jnp.broadcast_to(value, table.shape[1:])
    row = lax.broadcasted_iota(jnp.int32, (8, ROWS), 0)
    column = lax.broadcasted_iota(jnp.int32, (8, ROWS), 1)
    whole = jnp.zeros((8, ROWS), jnp.float32)
    for (i, j), value in factor.items():
        whole = jnp.where((row == i) & (column == j), value, whole)
    factor_out[...] = whole[:order, :order]

    def mul(n, x):
        return table[n][None] * x

    deep = 16 if ny % 16 == 0 else 8

    def tile(p, t):
        rows = pl.ds(pl.multiple_of(t * deep, deep), deep)
        for q in range(0, nz, ROWS):
            lanes = slice(q, q + ROWS)
            load = lambda x: x.reshape(deep // 8, 8, ROWS)
            fields = [load(v[k, p, rows, lanes]) for k in range(order)]
            for k in range(order):
                total = None
                for j in range(k + 1):
                    term = mul(pairs.index((j, k)), fields[j])
                    total = term if total is None else total + term
                basis_v[k, p, rows, lanes] = total.reshape(deep, ROWS)
            total = mul(tail, load(w[0, p, rows, lanes]))
            for k in range(1, steps):
                total = total + mul(tail + k, load(w[k, p, rows, lanes]))
            sol_v[p, rows, lanes] = total.reshape(deep, ROWS)
            total = mul(tail + steps, fields[0])
            for j in range(1, order):
                total = total + mul(tail + steps + j, fields[j])
            res_v[p, rows, lanes] = total.reshape(deep, ROWS)

    def copies(p):
        return (
            pltpu.make_async_copy(basis_v.at[:, p], basis.at[:, p], sem.at[p, 0]),
            pltpu.make_async_copy(sol_v.at[p], solution_out.at[p], sem.at[p, 1]),
            pltpu.make_async_copy(res_v.at[p], residual.at[p], sem.at[p, 2]),
        )

    def plane(p, c):
        def inner(t, d):
            tile(p, t)
            return d

        lax.fori_loop(0, ny // deep, inner, 0)
        for copy in copies(p):
            copy.start()
        return c

    def finish(p, c):
        for copy in copies(p):
            copy.wait()
        return c

    lax.fori_loop(0, nx, plane, 0)
    lax.fori_loop(0, nx, finish, 0)


def device_body(n_gx, n_gy, rhs, coefs, shifts):
    steps = shifts.shape[0]
    order = steps + 1
    nx, ny, nz = rhs.shape
    f32 = jnp.float32
    grown = (nx + 2, ny + 2 * PAD, nz)
    half = -(-(order * (order + 1) // 2) // 16) * 8
    pieces = 4 if ny % 32 == 0 else 1
    hbm = pl.BlockSpec(memory_space=pltpu.HBM)
    any_space = pl.BlockSpec(memory_space=pl.ANY)
    vmem = pl.BlockSpec(memory_space=pltpu.VMEM)
    dma = pltpu.SemaphoreType.DMA
    halo = 4 * steps
    rhs = pltpu.with_memory_space_constraint(rhs, pltpu.HBM)
    coefs = pltpu.with_memory_space_constraint(coefs, pltpu.HBM)
    shifts = pltpu.with_memory_space_constraint(shifts, pltpu.HBM)
    v, w, gram = pl.pallas_call(
        functools.partial(basis_kernel, n_gx, n_gy),
        out_shape=(
            jax.ShapeDtypeStruct((order, nx, ny, nz), f32),
            jax.ShapeDtypeStruct((steps, nx, ny, nz), f32),
            jax.ShapeDtypeStruct((2 * half, ROWS), f32),
        ),
        in_specs=[hbm, hbm, hbm],
        out_specs=(any_space, any_space, vmem),
        scratch_shapes=[
            pltpu.VMEM((order,) + grown, f32),
            pltpu.VMEM((steps,) + grown, f32),
            pltpu.VMEM(coefs.shape, f32),
            pltpu.VMEM((2 * half, ROWS), f32),
            pltpu.VMEM((n_gx, half, ROWS), f32),
            pltpu.VMEM((n_gy, half, ROWS), f32),
            pltpu.SMEM(shifts.shape, f32),
            pltpu.VMEM((halo, nx, nz), f32),
            pltpu.VMEM((halo, nx, nz), f32),
            dma((4,)),
            dma((2, order)),
            dma((halo * pieces,)),
            dma((halo * pieces,)),
            dma((halo,)),
            dma((halo,)),
            dma((n_gx,)),
            dma((n_gx,)),
            dma((n_gy,)),
            dma((n_gy,)),
        ],
        compiler_params=pltpu.CompilerParams(
            collective_id=0, has_side_effects=True, vmem_limit_bytes=32 * 2**20
        ),
        name="basis",
    )(shifts, rhs, coefs)

    cells = float(nx * ny * nz * n_gx * n_gy)
    return pl.pallas_call(
        functools.partial(combine_kernel, cells),
        out_shape=(
            jax.ShapeDtypeStruct((order, nx, ny, nz), f32),
            jax.ShapeDtypeStruct((order, order), f32),
            jax.ShapeDtypeStruct((nx, ny, nz), f32),
            jax.ShapeDtypeStruct((nx, ny, nz), f32),
        ),
        in_specs=[vmem, vmem, vmem],
        out_specs=(hbm, vmem, hbm, hbm),
        scratch_shapes=[
            pltpu.VMEM((order * (order + 1) // 2 + steps + order, 8, ROWS), f32),
            pltpu.VMEM((order, nx, ny, nz), f32),
            pltpu.VMEM((nx, ny, nz), f32),
            pltpu.VMEM((nx, ny, nz), f32),
            dma((nx, 3)),
        ],
        compiler_params=pltpu.CompilerParams(vmem_limit_bytes=32 * 2**20),
        name="combine",
    )(gram, v, w)


def solution(mesh):
    placed = (P("gx", "gy", None), P(None, "gx", "gy", None), P())
    return jax.shard_map(
        functools.partial(device_body, mesh.shape["gx"], mesh.shape["gy"]),
        mesh=mesh,
        in_specs=placed,
        out_specs=(P(None, "gx", "gy", None), P(), P("gx", "gy", None), P("gx", "gy", None)),
        check_vma=False,
    )
```
